32 devices in a mesh: groups: 2 (over y), ctx: 8 (over z, x), head: 2 (over core).
Axes of the slice: x: 2, y: 2, z: 4, core: 2. Of those that a mesh axis runs over, the one named last changes fastest.
Arguments:
- query_latent: bfloat16 [16, 64, 576], P(('groups', 'ctx'), 'head'), parts along dimension 0, may hold values from -9 to 9
- latent_codes: bfloat16 [4096, 576], P(('groups', 'ctx')), parts along dimension 0, may hold values from -6 to 6
- latent_scales: float32 [4096, 9], P(('groups', 'ctx')), parts along dimension 0, may hold values from 0.5 to 2
- valid_lengths: int32 [16], P(('groups', 'ctx')), parts along dimension 0, may hold values from 1 to 256
- query_position: int32 [16], P('groups'), parts along dimension 0, may hold values from 0 to 2047
- value_up: bfloat16 [64, 512, 128], P('head'), may hold values from -1 to 1
- out_codes: bfloat16 [8192, 7168], P('head', 'ctx'), may hold values from -0.0625 to 0.0625
- out_scales: float32 [7168], P('ctx'), may hold values from 0.5 to 2
Outputs:
- attention: bfloat16 [16, 8192], P(('groups', 'ctx'), 'head'), parts along dimension 0
- projected: bfloat16 [16, 7168], P(('groups', 'head'), 'ctx'), parts along dimension 0
The draws below stay inside these ranges and needn't reach their ends.
There are 2 independent parts, one for each index of `groups`. The reference program is written for one: setup_inputs(seed, part) draws one part's arguments, and reference() takes and returns one part's arrays. A program takes and returns all parts, laid end to end along the dimension named above; an argument that names none is the same for every part. Nothing has to cross between parts.
All inputs are finite; a program needn't handle non-finite values.
Results may differ from the reference program's by a relative error of at most 0.011.
Values may be sent and summed in bfloat16 or wider, within the bound.
No kernel may reach another device: no remote copies, remote signals or barrier semaphores. Data moves between devices by JAX's collectives and lax.ppermute only.
A program may use at most 128 MiB of HBM per device.

```python
import math
import jax
import jax.numpy as jnp
from jax import lax

D = 7168
LAT_NOPE = 512
ROPE = 64
VHEAD = 128
QK_NOPE = 128
HEADS = 64
SBLK = 64
CTX_DEV = 256
LAT = 576
NBLK = 9
CONTEXT = 2048
QTOK = 8
RANKS = 8
N_CTX = 8


def draw_latent_codes(key, part):
    codes = jnp.clip(jax.random.normal(jax.random.fold_in(key, 201), (CONTEXT, LAT), jnp.float32), -6.0, 6.0)
    return codes.astype(jnp.bfloat16)


def draw_query_latent(key, part):
    values = jnp.clip(1.5 * jax.random.normal(jax.random.fold_in(key, 301), (QTOK, HEADS, LAT), jnp.float32), -9.0, 9.0)
    return values.astype(jnp.bfloat16)


def place_ends(entries, own_key, low, top_value):
    longest = entries.shape.index(max(entries.shape))
    spots = []
    for shift in (0, 1):
        where = [jax.random.randint(jax.random.fold_in(own_key, axis), (), 0, length) for axis, length in enumerate(entries.shape)]
        where[longest] = (where[longest] + shift) % entries.shape[longest]
        spots.append(tuple(where))
    return entries.at[spots[0]].set(low).at[spots[1]].set(top_value)


def level_of(key, shape, pieces, smallest, top_value):
    loudness, own = 1.0, jax.random.fold_in(key, 6)
    for dim, shards_of in pieces:
        draws = jnp.exp(jax.random.uniform(jax.random.fold_in(own, dim), (shards_of,), jnp.float32, smallest / len(pieces), top_value / len(pieces)))
        loudness = loudness * jnp.repeat(draws, shape[dim] // shards_of).reshape([-1 if axis == dim else 1 for axis in range(len(shape))])
    return loudness


def gaussian(key, dims, width, reach, split=(), kind=jnp.bfloat16):
    level = level_of(key, dims, split, -0.22, 0.18) if split else 1.0
    drawn = jax.random.normal(key, dims, jnp.float32) * width * level
    return jnp.minimum(jnp.maximum(drawn, -reach), reach).astype(kind)


def setup_inputs(seed: int = 0, part: int = 0) -> dict:
    streams_of = jax.random.split(jax.random.key(seed), 9)
    part_keys = jax.random.split(jax.random.fold_in(streams_of[8], part), 9)
    query_latent = draw_query_latent(jax.random.fold_in(jax.random.fold_in(streams_of[8], part), 71), part)
    latent_codes = draw_latent_codes(jax.random.fold_in(jax.random.fold_in(streams_of[8], part), 71), part)
    latent_scales = jnp.clip(jnp.exp(math.log(2.0) - 1.3862944 * jax.random.uniform(part_keys[2], (CONTEXT, NBLK), jnp.float32) ** level_of(part_keys[2], (CONTEXT, NBLK), ((0, 8),), -0.2, 0.2)), 0.5, 2.0)
    valid_lengths = place_ends(jax.random.randint(part_keys[3], (RANKS,), 1, CTX_DEV + 1), jax.random.fold_in(part_keys[3], 1), 1, CTX_DEV).astype(jnp.int32)
    query_position = place_ends(jax.random.randint(part_keys[4], (QTOK,), 0, CONTEXT), jax.random.fold_in(part_keys[4], 1), 0, CONTEXT - 1).astype(jnp.int32)
    value_up = gaussian(streams_of[5], (HEADS, LAT_NOPE, VHEAD), (LAT_NOPE // 16) ** -0.5, 1.0, ((0, 2),))
    out_codes = gaussian(streams_of[6], (HEADS * VHEAD, D), (HEADS * VHEAD) ** -0.5, 0.0625, ((0, 2), (1, 8)))
    out_scales = jnp.clip(jnp.exp(math.log(2.0) - 1.3862944 * jax.random.uniform(streams_of[7], (D,), jnp.float32) ** level_of(streams_of[7], (D,), ((0, 8),), -0.2, 0.2)), 0.5, 2.0)
    return dict(query_latent=query_latent, latent_codes=latent_codes, latent_scales=latent_scales, valid_lengths=valid_lengths, query_position=query_position, value_up=value_up, out_codes=out_codes, out_scales=out_scales)


def reference(query_latent, latent_codes, latent_scales, valid_lengths, query_position, value_up, out_codes, out_scales):
    latent = (latent_codes.astype(jnp.float32).reshape(CONTEXT, NBLK, SBLK) * latent_scales[:, :, None]).reshape(CONTEXT, LAT).astype(jnp.bfloat16)
    key_pos = jnp.arange(CONTEXT, dtype=jnp.int32)
    owner = key_pos // CTX_DEV
    usable = (key_pos % CTX_DEV) < valid_lengths[owner]
    allowed = usable[None, :] & (key_pos[None, :] <= query_position[:, None])
    softmax_scale = (QK_NOPE + ROPE) ** -0.5
    nope_shards = latent[:, :LAT_NOPE].astype(jnp.float32).reshape(N_CTX, CTX_DEV, LAT_NOPE)

    def one_head(inputs):
        query_head, up_head = inputs
        logits = jnp.dot(query_head, latent.T, preferred_element_type=jnp.float32) * softmax_scale
        logits = jnp.where(allowed, logits, -jnp.inf)
        maxima = jnp.max(logits, axis=1, keepdims=True)
        weights = jnp.exp(logits - maxima)
        totals = jnp.sum(weights, axis=1)
        rounded = lax.optimization_barrier(weights.astype(jnp.bfloat16))
        rounded = rounded.astype(jnp.float32).reshape(QTOK, N_CTX, CTX_DEV)
        partial_mix = lax.optimization_barrier(jnp.einsum("qrk,rkd->rqd", rounded, nope_shards).astype(jnp.bfloat16))
        numerators = jnp.einsum("rqd,dv->qv", partial_mix.astype(jnp.float32), up_head.astype(jnp.float32))
        return numerators / totals[:, None]

    head_outputs = lax.map(one_head, (jnp.transpose(query_latent, (1, 0, 2)), value_up))
    attention = jnp.transpose(head_outputs, (1, 0, 2)).reshape(QTOK, HEADS * VHEAD).astype(jnp.bfloat16)
    projected = (jnp.dot(attention, out_codes, preferred_element_type=jnp.float32) * out_scales[None, :]).astype(jnp.bfloat16)
    return attention, projected
```

```python
import functools

import jax
import jax.numpy as jnp
from jax import lax
from jax.sharding import PartitionSpec as P

LAT_NOPE = 512
ROPE = 64
QK_NOPE = 128
BF16 = jnp.bfloat16
F32 = jnp.float32
EMPTY = -1e30


def flip(x, size, distance):
    return lax.ppermute(x, "ctx", [(i, i ^ distance) for i in range(size)])


def digits_of(count):
    digits, stride = [], 1
    while stride < count:
        radix = 4 if stride * 4 <= count else 2
        digits.append((stride, radix))
        stride *= radix
    return digits


def pieces(x):
    high = x.astype(BF16)
    rest = x - high.astype(F32)
    middle = rest.astype(BF16)
    low = (rest - middle.astype(F32)).astype(BF16)
    return high, middle, low


def shards(
    size,
    query_latent,
    latent_codes,
    latent_scales,
    valid_lengths,
    query_position,
    value_up,
    out_codes,
    out_scales,
):
    key_count, width = latent_codes.shape
    block_count = latent_scales.shape[1]
    _, heads, _ = query_latent.shape
    value_width = value_up.shape[2]
    far = size // 2
    index = lax.axis_index("ctx")
    near_index, far_index = index % 2, index // 2

    latent = (
        (
            latent_codes.T.astype(F32).reshape(block_count, width // block_count, key_count)
            * latent_scales.T[:, None, :]
        )
        .reshape(width, key_count)
        .astype(BF16)
    )
    dead = (jnp.arange(key_count, dtype=jnp.int32) >= valid_lengths[0]).astype(BF16)
    keys = jnp.concatenate([latent, jnp.broadcast_to(dead[None, :], (16, key_count))])
    keys = jnp.concatenate([keys, flip(keys, size, 1)], axis=1)

    queries = query_latent
    for stride, radix in digits_of(far):
        queries = jnp.concatenate(
            [queries] + [flip(queries, size, 2 * stride * k) for k in range(1, radix)]
        )
    order = jnp.arange(far, dtype=jnp.int32) ^ far_index
    position = query_position.reshape(far, 2)[:, near_index][order]

    logits = jnp.einsum("khc,cp->khp", queries, keys[:width], preferred_element_type=F32)
    logits = logits * (QK_NOPE + ROPE) ** (-0.5)
    slots = jnp.arange(key_count, dtype=jnp.int32)
    key_pos = jnp.concatenate([index * key_count + slots, (index ^ 1) * key_count + slots])
    allowed = (keys[width] == 0)[None, :] & (key_pos[None, :] <= position[:, None])
    scores = jnp.where(allowed[:, None, :], logits, EMPTY)
    maxima = jnp.max(scores, axis=2)
    weights = jnp.where(allowed[:, None, :], jnp.exp(scores - maxima[:, :, None]), 0.0)
    totals = jnp.sum(weights, axis=2)
    mix = jnp.einsum(
        "khp,cp->khc", weights.astype(BF16), keys[:LAT_NOPE], preferred_element_type=F32
    ).astype(BF16)
    values = jnp.einsum("khc,hcv->khv", mix, value_up, preferred_element_type=F32)
    any_key = totals > 0
    values = values / jnp.where(any_key, totals, 1.0)[:, :, None]
    logsum = jnp.where(any_key, maxima + jnp.log(jnp.where(any_key, totals, 1.0)), EMPTY)

    for stride, radix in digits_of(far):
        sent = jnp.concatenate(
            [values.astype(BF16).reshape(far, heads * value_width), *pieces(logsum)], axis=1
        )
        parts = [(values, logsum)]
        for k in range(1, radix):
            got = flip(sent, size, 2 * stride * k)
            got = jnp.concatenate([got[j ^ (stride * k)][None] for j in range(far)])
            stats = got[:, heads * value_width :].astype(F32).reshape(far, 3, heads)
            parts.append(
                (
                    got[:, : heads * value_width].astype(F32).reshape(far, heads, value_width),
                    stats[:, 0] + stats[:, 1] + stats[:, 2],
                )
            )
        top = functools.reduce(jnp.maximum, [s for _, s in parts])
        shares = [jnp.exp(s - top) for _, s in parts]
        total = sum(shares)
        values = sum(v * w[:, :, None] for (v, _), w in zip(parts, shares)) / total[:, :, None]
        logsum = top + jnp.log(total)

    attention = values.astype(BF16).reshape(far, heads * value_width)
    both = jnp.concatenate([attention, flip(attention, size, 1)])
    projected = jnp.dot(both, out_codes, preferred_element_type=F32)
    projected = projected.reshape(2, far, -1)
    projected = jnp.where(near_index == 1, projected[::-1], projected).transpose(1, 0, 2)
    bit = 1
    while bit < far:
        shaped = projected.reshape(far // (2 * bit), 2, bit, 2, -1)
        projected = jnp.where((far_index & bit) != 0, shaped[:, ::-1], shaped)
        bit *= 2
    projected = projected.reshape(2, far, -1)
    head = lax.axis_index("head")
    swapped = lax.ppermute(
        jnp.where(head == 1, projected[0], projected[1]), "head", [(0, 1), (1, 0)]
    )
    summed = jnp.where(head == 1, projected[1], projected[0]) + swapped
    return attention[:1], (summed * out_scales[None, :]).astype(BF16)


def solution(mesh):
    return jax.shard_map(
        functools.partial(shards, mesh.shape["ctx"]),
        mesh=mesh,
        in_specs=(
            P(("groups", "ctx"), "head", None),
            P(("groups", "ctx"), None),
            P(("groups", "ctx"), None),
            P(("groups", "ctx")),
            P("groups"),
            P("head", None, None),
            P("head", "ctx"),
            P("ctx"),
        ),
        out_specs=(P(("groups", "ctx"), "head"), P(("groups", "head"), "ctx")),
        check_vma=False,
    )
```
